32 devices in a mesh: row: 4 (over y, x), col: 8 (over z, core).
Axes of the slice: x: 2, y: 2, z: 4, core: 2. Of those that a mesh axis runs over, the one named last changes fastest.
Arguments:
- node_features: bfloat16 [4096, 1024], P(('row', 'col')), may hold values from -6 to 6
- norm_gain: float32 [1024], replicated, may hold values from 0.5 to 1.5
- w_query: bfloat16 [1024, 1024], replicated, may hold values from -0.1875 to 0.1875
- w_keyvalue: bfloat16 [1024, 2048], replicated, may hold values from -0.1875 to 0.1875
- w_out: bfloat16 [1024, 1024], replicated, may hold values from -0.1875 to 0.1875
- bias_table: float32 [32, 8], replicated, may hold values from -4 to 4
- edge_slope: float32 [8], replicated, may hold values from 0.5 to 1.5
- pair_blocks: int32 [4, 8, 2, 16], P('row', 'col'), may hold values from -1 to 7, as said below
- bucket_ids: int32 [4, 8, 16, 128, 128], P('row', 'col'), may hold values from 0 to 31
- edge_weight: bfloat16 [4, 8, 4, 4, 128, 128], P('row', 'col'), may hold values from -4 to 240
Outputs:
- node_out: bfloat16 [4096, 1024], P(('row', 'col'))
The draws below stay inside these ranges and needn't reach their ends.
Inputs may be any that keep to these rules, and one draw needn't show every extreme that they name: `pair_blocks`: slots of a tile with query block -1 are empty and name key block 0. The listed pairs of a tile are distinct; each tile (r, c) lists, among the slots from t = r, every block of node shard r * 8 + c paired with itself. Up to 4 slots from one owner to one row range are used, and some tile uses all 16 of its slots.
All inputs are finite; a program needn't handle non-finite values.
Results may differ from the reference program's by a relative error of at most 0.005.
Values may be sent and summed in bfloat16 or wider, within the bound.
A program may use at most 256 MiB of HBM per device.

```python
import math
import jax
import jax.numpy as jnp
from jax import lax

D = 1024
H = 8
BLK = 128
NB = 32
NODES_DEV = 128
KB_DEV = 1
QB_ROW = 8
CAP = 4
SLOTS = 16
NODES = 4096
N_ROW = 4
N_COL = 8


def draw_edge_weight(key, part):
    full_shape = (N_ROW, N_COL, N_ROW, CAP, BLK, BLK)
    return jnp.clip(jax.random.normal(jax.random.fold_in(key, 6), full_shape, jnp.float32), -4.0, 4.0).astype(jnp.bfloat16)


def draw_pair_blocks(key, part):
    cand_count = QB_ROW * KB_DEV
    group_shape = (N_ROW, N_COL, N_ROW)
    cand_index = jnp.arange(cand_count, dtype=jnp.int32)
    rand_score = jax.random.randint(jax.random.fold_in(key, 11), group_shape + (cand_count,), 0, 1 << 16)
    order_key = rand_score * cand_count + cand_index
    dest_row = jnp.arange(N_ROW, dtype=jnp.int32).reshape(N_ROW, 1, 1, 1)
    col_index = jnp.arange(N_COL, dtype=jnp.int32).reshape(1, N_COL, 1, 1)
    source_row = jnp.arange(N_ROW, dtype=jnp.int32).reshape(1, 1, N_ROW, 1)
    query_part = cand_index // KB_DEV
    key_part = cand_index % KB_DEV
    diagonal = (dest_row == source_row) & (query_part == col_index * KB_DEV + key_part)
    order_key = jnp.where(diagonal, cand_index - cand_count, order_key)
    picked = jnp.argsort(order_key, axis=-1)[..., :CAP].astype(jnp.int32)
    live_count = jax.random.randint(jax.random.fold_in(key, 12), group_shape, 1, CAP + 1)
    full_row = jax.random.randint(jax.random.fold_in(key, 13), (), 0, N_ROW)
    full_col = jax.random.randint(jax.random.fold_in(key, 14), (), 0, N_COL)
    dest_grid = dest_row[..., 0]
    col_grid = col_index[..., 0]
    source_grid = source_row[..., 0]
    live_count = jnp.where((dest_grid == full_row) & (col_grid == full_col), CAP, live_count)
    live_count = jnp.where(dest_grid == source_grid, jnp.maximum(live_count, KB_DEV), live_count)
    slot_index = jnp.arange(CAP, dtype=jnp.int32)
    slot_live = slot_index < live_count[..., None]
    query_block = jnp.where(slot_live, picked // KB_DEV, -1)
    key_block = jnp.where(slot_live, picked % KB_DEV, 0)
    stacked = jnp.stack([query_block, key_block], axis=2)
    return stacked.reshape(N_ROW, N_COL, 2, N_ROW * CAP).astype(jnp.int32)


def set_ends(array, key, smallest, largest):
    longest = array.shape.index(max(array.shape))
    spots = []
    for shift in (0, 1):
        where = [jax.random.randint(jax.random.fold_in(key, axis), (), 0, length) for axis, length in enumerate(array.shape)]
        where[longest] = (where[longest] + shift) % array.shape[longest]
        spots.append(tuple(where))
    return array.at[spots[0]].set(smallest).at[spots[1]].set(largest)


def steps_of(rng, dims, pieces, smallest, top_value):
    level = 1.0
    for dim, parts in pieces:
        heights = jax.random.uniform(jax.random.fold_in(jax.random.fold_in(rng, 6), dim), (parts,), jnp.float32, smallest / len(pieces), top_value / len(pieces))
        level = level * jnp.repeat(jnp.exp(heights), dims[dim] // parts).reshape((-1,) + (1,) * (len(dims) - 1 - dim))
    return level


def gaussian(key, extent, width, bound, cuts=(), kind=jnp.bfloat16):
    drawn = width * jax.random.normal(key, extent, jnp.float32)
    if cuts:
        drawn = drawn * steps_of(key, extent, cuts, -0.22, 0.18)
    return jnp.clip(drawn, -bound, bound).astype(kind)


def setup_inputs(seed: int = 0) -> dict:
    key_of = jax.random.split(jax.random.key(seed), 11)
    node_features = gaussian(key_of[0], (NODES, D), 1.0, 6.0, ((0, 32),))
    norm_gain = jnp.clip(1.0 + 0.1 * jax.random.normal(key_of[1], (D,), jnp.float32), 0.5, 1.5)
    w_query = gaussian(key_of[2], (D, D), D ** -0.5, 0.1875)
    w_keyvalue = gaussian(key_of[3], (D, 2 * D), D ** -0.5, 0.1875)
    w_out = gaussian(key_of[4], (D, D), D ** -0.5, 0.1875)
    bias_table = gaussian(key_of[5], (NB, H), 1.0, 4.0, (), jnp.float32)
    edge_slope = jnp.clip(jnp.exp(jax.random.uniform(key_of[6], (H,), jnp.float32, math.log(0.5), math.log(1.5))), 0.5, 1.5)
    pair_blocks = draw_pair_blocks(jax.random.fold_in(key_of[10], 71), 0)
    bucket_ids = set_ends(jax.random.randint(key_of[8], (N_ROW, N_COL, SLOTS, BLK, BLK), 0, NB), jax.random.fold_in(key_of[8], 1), 0, NB - 1).astype(jnp.int32)
    edge_weight = draw_edge_weight(jax.random.fold_in(key_of[10], 71), 0)
    return {"node_features": node_features, "norm_gain": norm_gain, "w_query": w_query, "w_keyvalue": w_keyvalue, "w_out": w_out, "bias_table": bias_table, "edge_slope": edge_slope, "pair_blocks": pair_blocks, "bucket_ids": bucket_ids, "edge_weight": edge_weight}


EPSILON = 1e-05
LOW_FLOOR = -1e+30

def normalize(features, gain_vec):
    as_float = features.astype(jnp.float32)
    centered = as_float - lax.optimization_barrier(jnp.mean(as_float, axis=-1, keepdims=True))
    variance = lax.optimization_barrier(jnp.mean(centered * centered, axis=-1, keepdims=True))
    return (centered * lax.rsqrt(variance + EPSILON) * gain_vec).astype(jnp.bfloat16)

def slot_terms(query_range, key_group, value_group, query_block, key_block, tile_weights, tile_buckets, bias_table, edge_slope):
    head_count = edge_slope.shape[0]
    head_dim = query_range.shape[1] // head_count
    query_start = (jnp.maximum(query_block, 0) * BLK).astype(jnp.int32)
    key_start = (key_block * BLK).astype(jnp.int32)
    query_tile = lax.dynamic_slice_in_dim(query_range, query_start, BLK, 0).astype(jnp.float32).reshape(BLK, head_count, head_dim)
    key_tile = lax.dynamic_slice_in_dim(key_group, key_start, BLK, 0).astype(jnp.float32).reshape(BLK, head_count, head_dim)
    value_tile = lax.dynamic_slice_in_dim(value_group, key_start, BLK, 0).astype(jnp.float32).reshape(BLK, head_count, head_dim)
    raw_score = jnp.einsum('ihd,jhd->hij', query_tile, key_tile) * head_dim ** (-0.5)
    raw_score = raw_score + jnp.transpose(bias_table[tile_buckets], (2, 0, 1))
    raw_score = raw_score + edge_slope[:, None, None] * tile_weights.astype(jnp.float32)[None]
    row_max = lax.optimization_barrier(jnp.max(raw_score, axis=-1))
    rounded = lax.optimization_barrier(jnp.exp(raw_score - row_max[:, :, None]).astype(jnp.bfloat16))
    prob_vals = rounded.astype(jnp.float32)
    row_sum = lax.optimization_barrier(jnp.sum(prob_vals, axis=-1))
    weighted = jnp.einsum('hij,jhd->ihd', prob_vals, value_tile)
    return (row_max, row_sum, weighted)

def tile_partials(query_range, key_group, value_group, pair_table, edge_values, bucket_tiles, bias_table, edge_slope):
    range_rows = query_range.shape[0]
    head_count = edge_slope.shape[0]
    head_dim = query_range.shape[1] // head_count
    slot_count = pair_table.shape[1]
    slot_cap = slot_count // N_ROW
    key_blocks = NODES_DEV // BLK
    initial = (jnp.full((range_rows, head_count), LOW_FLOOR, jnp.float32), jnp.zeros((range_rows, head_count), jnp.float32), jnp.zeros((range_rows, head_count, head_dim), jnp.float32))

    def advance(carry, inputs):
        max_all, sum_all, out_all = carry
        query_block, key_part, tile_weights, tile_buckets, slot_index = inputs
        key_block = key_part + slot_index // slot_cap * key_blocks
        row_max, row_sum, weighted = slot_terms(query_range, key_group, value_group, query_block, key_block, tile_weights, tile_buckets, bias_table, edge_slope)
        row_start = (jnp.maximum(query_block, 0) * BLK).astype(jnp.int32)
        old_max = lax.dynamic_slice_in_dim(max_all, row_start, BLK, 0)
        old_sum = lax.dynamic_slice_in_dim(sum_all, row_start, BLK, 0)
        old_out = lax.dynamic_slice_in_dim(out_all, row_start, BLK, 0)
        new_max = jnp.maximum(old_max, row_max.T)
        left_scale = jnp.exp(old_max - new_max)
        right_scale = jnp.exp(row_max.T - new_max)
        new_sum = old_sum * left_scale + row_sum.T * right_scale
        new_out = old_out * left_scale[:, :, None] + weighted * right_scale[:, :, None]
        slot_live = query_block >= 0
        new_max = jnp.where(slot_live, new_max, old_max)
        new_sum = jnp.where(slot_live, new_sum, old_sum)
        new_out = jnp.where(slot_live, new_out, old_out)
        max_all = lax.dynamic_update_slice_in_dim(max_all, new_max, row_start, 0)
        sum_all = lax.dynamic_update_slice_in_dim(sum_all, new_sum, row_start, 0)
        out_all = lax.dynamic_update_slice_in_dim(out_all, new_out, row_start, 0)
        return ((max_all, sum_all, out_all), None)
    carry, _ = lax.scan(advance, initial, (pair_table[0], pair_table[1], edge_values, bucket_tiles, jnp.arange(slot_count, dtype=jnp.int32)))
    return carry

def reference(node_features, norm_gain, w_query, w_keyvalue, w_out, bias_table, edge_slope, pair_blocks, bucket_ids, edge_weight):
    model_width = node_features.shape[1]
    head_count = edge_slope.shape[0]
    head_dim = model_width // head_count
    normalized = normalize(node_features, norm_gain)
    queries = jnp.dot(normalized, w_query, preferred_element_type=jnp.float32).astype(jnp.bfloat16)
    key_value = jnp.dot(normalized, w_keyvalue, preferred_element_type=jnp.float32).astype(jnp.bfloat16)
    range_rows = N_COL * NODES_DEV
    query_rows = queries.reshape(N_ROW, range_rows, model_width)
    grouped = key_value.reshape(N_ROW, N_COL, NODES_DEV, 2 * model_width)
    slot_count = N_ROW * CAP

    def row_range(row_index):
        query_range = query_rows[row_index]

        def one_col(carry, col_index):
            key_group = grouped[:, col_index].reshape(N_ROW * NODES_DEV, 2 * model_width)
            edge_values = edge_weight[:, col_index, row_index].reshape(slot_count, BLK, BLK)
            col_max, col_sum, col_out = tile_partials(query_range, key_group[:, :model_width], key_group[:, model_width:], pair_blocks[row_index, col_index], edge_values, bucket_ids[row_index, col_index], bias_table, edge_slope)
            max_all, sum_all, out_all = carry
            new_max = jnp.maximum(max_all, col_max)
            left_scale = jnp.exp(max_all - new_max)
            right_scale = jnp.exp(col_max - new_max)
            return ((new_max, sum_all * left_scale + col_sum * right_scale, out_all * left_scale[:, :, None] + col_out * right_scale[:, :, None]), None)
        initial = (jnp.full((range_rows, head_count), LOW_FLOOR, jnp.float32), jnp.zeros((range_rows, head_count), jnp.float32), jnp.zeros((range_rows, head_count, head_dim), jnp.float32))
        (max_all, sum_all, out_all), _ = lax.scan(one_col, initial, jnp.arange(N_COL, dtype=jnp.int32))
        return (out_all / sum_all[:, :, None]).astype(jnp.bfloat16).reshape(range_rows, model_width)
    attention = lax.map(row_range, jnp.arange(N_ROW, dtype=jnp.int32)).reshape(N_ROW * range_rows, model_width)
    update = jnp.dot(attention, w_out, preferred_element_type=jnp.float32)
    return (node_features.astype(jnp.float32) + update).astype(jnp.bfloat16)
```

```python
import functools

import jax
import jax.numpy as jnp
from jax import lax
from jax.experimental import pallas as pl
from jax.experimental.pallas import tpu as pltpu
from jax.sharding import PartitionSpec as P

EPSILON = 1e-05
LOW_FLOOR = -1e30
CORES = 2
MESH = pl.DeviceIdType.MESH
VMEM_LIMIT = 60 * 2**20


def normalize(features, gain_vec):
    as_float = features.astype(jnp.float32)
    centered = as_float - jnp.mean(as_float, axis=-1, keepdims=True)
    variance = jnp.mean(centered * centered, axis=-1, keepdims=True)
    return (centered * lax.rsqrt(variance + EPSILON) * gain_vec).astype(jnp.bfloat16)


def greet(partners):
    barrier = pltpu.get_barrier_semaphore()
    for partner in partners:
        pl.semaphore_signal(barrier, inc=1, device_id=partner, device_id_type=MESH)
    pl.semaphore_wait(barrier, len(partners))


def exchange(n_row, n_chip, q_in, n_in, e_in, q_out, n_out, e_out, send_sem, recv_sem, own_sem):
    row, col = lax.axis_index("row"), lax.axis_index("col")
    chip, core = col // CORES, col % CORES
    sibling = (row, chip * CORES + (1 - core))
    chips = [(row, ((chip + k) % n_chip) * CORES + core) for k in range(1, n_chip)]
    rows = [((row + k) % n_row, col) for k in range(1, n_row)]
    greet(chips + [sibling] + rows)
    count = [0]

    def send(src, dst, where):
        spot = count[0]
        count[0] += 1
        copy = pltpu.make_async_remote_copy(
            src_ref=src,
            dst_ref=dst,
            send_sem=send_sem.at[spot],
            recv_sem=recv_sem.at[spot],
            device_id=where,
            device_id_type=MESH,
        )
        copy.start()
        return copy

    over_chips = [send(q_in, q_out.at[col], where) for where in chips]
    rest = [send(n_in, n_out.at[row], where) for where in rows]
    rest += [send(e_in.at[where[0]], e_out.at[row], where) for where in rows]
    rest.append(send(q_in, q_out.at[col], sibling))
    own = [
        pltpu.make_async_copy(q_in, q_out.at[col], own_sem.at[0]),
        pltpu.make_async_copy(n_in, n_out.at[row], own_sem.at[1]),
        pltpu.make_async_copy(e_in.at[row], e_out.at[row], own_sem.at[2]),
    ]
    for copy in own:
        copy.start()
    for k, copy in enumerate(over_chips, 1):
        copy.wait_recv()
        origin = ((chip + n_chip - k) % n_chip) * CORES + core
        rest.append(send(q_out.at[origin], q_out.at[origin], sibling))
    for copy in over_chips:
        copy.wait_send()
    for copy in rest:
        copy.wait()
    for copy in own:
        copy.wait()


def attend(
    slot_cap, scale, pairs, slope, table, q_ref, kv_ref, e_ref, b_ref, o_ref, l_ref, m_acc, s_acc, o_acc
):
    query_count, tile, width = q_ref.shape
    heads = l_ref.shape[1]
    dim = width // heads
    m_acc[...] = jnp.full(m_acc.shape, LOW_FLOOR, jnp.float32)
    s_acc[...] = jnp.zeros(s_acc.shape, jnp.float32)
    o_acc[...] = jnp.zeros(o_acc.shape, jnp.float32)
    ones = jnp.ones((tile, dim), jnp.bfloat16)

    def slot_step(slot, carry):
        query = pairs[0, slot]

        @pl.when(query >= 0)
        def _():
            key = pairs[1, slot] + slot // slot_cap
            buckets = b_ref[slot]
            edges = e_ref[slot].astype(jnp.float32)
            for h in range(heads):
                cols = slice(h * dim, (h + 1) * dim)
                vals = slice(width + h * dim, width + (h + 1) * dim)
                score = lax.dot_general(
                    q_ref[query, :, cols],
                    kv_ref[key, :, cols],
                    (((1,), (1,)), ((), ())),
                    preferred_element_type=jnp.float32,
                )
                entries = jnp.broadcast_to(table[h : h + 1, :], (tile, table.shape[1]))
                bias = jnp.take_along_axis(entries, buckets, axis=1, mode="promise_in_bounds")
                score = score * scale + bias + slope[h] * edges
                old_max = m_acc[query, h]
                new_max = jnp.maximum(old_max, jnp.max(score, axis=-1, keepdims=True))
                probs = jnp.exp(score - new_max).astype(jnp.bfloat16)
                both = jnp.dot(
                    probs,
                    jnp.concatenate([kv_ref[key, :, vals], ones], axis=1),
                    preferred_element_type=jnp.float32,
                )
                keep = jnp.exp(old_max - new_max)
                m_acc[query, h] = new_max
                o_acc[query, h] = o_acc[query, h] * keep + both[:, :dim]
                s_acc[query, h] = s_acc[query, h] * keep + both[:, dim:]

        return carry

    lax.fori_loop(0, pairs.shape[1], slot_step, 0)
    lane = lax.broadcasted_iota(jnp.int32, (tile, tile), 1)

    def finish(query, carry):
        packed = jnp.full((tile, tile), LOW_FLOOR, jnp.float32)
        for h in range(heads):
            total = s_acc[query, h]
            live = total > 0.0
            safe = jnp.where(live, total, 1.0)
            o_ref[query, :, h * dim : (h + 1) * dim] = (o_acc[query, h] / safe).astype(o_ref.dtype)
            level = jnp.where(live, m_acc[query, h] + jnp.log(safe), LOW_FLOOR)
            packed = jnp.where(lane == h, level, packed)
        l_ref[query] = packed.T[:heads]
        return carry

    lax.fori_loop(0, query_count, finish, 0)


def blend(levels, parts, heads):
    top = functools.reduce(jnp.maximum, levels)
    shares = [jnp.exp(level - top) for level in levels]
    total = functools.reduce(jnp.add, shares)
    weights = [(share / total).T for share in shares]
    dim = parts[0].shape[1] // heads
    out = []
    for h in range(heads):
        cols = slice(h * dim, (h + 1) * dim)
        terms = [w[:, h : h + 1] * part[:, cols].astype(jnp.float32) for w, part in zip(weights, parts)]
        out.append(functools.reduce(jnp.add, terms))
    return out, top + jnp.log(total)


def combine(
    n_chip, o_ref, l_ref, a_ref, sib_o, sib_l, mix_o, mix_l, got_o, got_l, send_sem, recv_sem
):
    row, col = lax.axis_index("row"), lax.axis_index("col")
    chip, core = col // CORES, col % CORES
    heads = l_ref.shape[1]
    dim = o_ref.shape[2] // heads
    sibling = (row, chip * CORES + (1 - core))
    chips = [(row, ((chip + k) % n_chip) * CORES + core) for k in range(1, n_chip)]
    greet(chips + [sibling])

    def send(spot, src, dst, where):
        copy = pltpu.make_async_remote_copy(
            src_ref=src,
            dst_ref=dst,
            send_sem=send_sem.at[spot],
            recv_sem=recv_sem.at[spot],
            device_id=where,
            device_id_type=MESH,
        )
        copy.start()
        return copy

    order = list(range(1, n_chip)) + [0]
    to_sibling = {}
    for k in order:
        theirs = ((chip + k) % n_chip) * CORES + (1 - core)
        to_sibling[k] = [
            send(4 * k, l_ref.at[theirs], sib_l.at[k], sibling),
            send(4 * k + 1, o_ref.at[theirs], sib_o.at[k], sibling),
        ]
    over = []

    def push(k):
        over.append(send(4 * k + 2, mix_l.at[k], got_l.at[k], chips[k - 1]))
        over.append(send(4 * k + 3, mix_o.at[k], got_o.at[k], chips[k - 1]))

    for k in range(1, n_chip):
        for copy in to_sibling[k]:
            copy.wait_recv()
        mine = ((chip + k) % n_chip) * CORES + core
        out, level = blend([l_ref[mine], sib_l[k]], [o_ref[mine], sib_o[k]], heads)
        for h in range(heads):
            mix_o[k, :, h * dim : (h + 1) * dim] = out[h].astype(mix_o.dtype)
        mix_l[k] = level
        push(k)
    for copy in to_sibling[0]:
        copy.wait_recv()
    for copy in over:
        copy.wait_recv()
    levels = [l_ref[col], sib_l[0]] + [got_l[k] for k in range(1, n_chip)]
    parts = [o_ref[col], sib_o[0]] + [got_o[k] for k in range(1, n_chip)]
    out, _ = blend(levels, parts, heads)
    for h in range(heads):
        a_ref[:, h * dim : (h + 1) * dim] = out[h].astype(a_ref.dtype)
    for copies in to_sibling.values():
        for copy in copies:
            copy.wait_send()
    for copy in over:
        copy.wait_send()


def local(
    n_row,
    n_col,
    node_features,
    norm_gain,
    w_query,
    w_keyvalue,
    w_out,
    bias_table,
    edge_slope,
    pair_blocks,
    bucket_ids,
    edge_weight,
):
    tile, width = node_features.shape
    heads = edge_slope.shape[0]
    dim = width // heads
    n_chip = n_col // CORES
    slot_cap = edge_weight.shape[3]
    slots = n_row * slot_cap
    bf16, f32 = jnp.bfloat16, jnp.float32
    vmem = pl.BlockSpec(memory_space=pltpu.VMEM)
    smem = pl.BlockSpec(memory_space=pltpu.SMEM)
    hbm = pl.BlockSpec(memory_space=pl.ANY)

    normalized = normalize(node_features, norm_gain)
    queries = jnp.dot(normalized, w_query, preferred_element_type=f32).astype(bf16)
    copies = 2 * (n_chip - 1) + 2 * (n_row - 1) + 1
    query_range, norm_group, edge_values = pl.pallas_call(
        functools.partial(exchange, n_row, n_chip),
        out_shape=(
            jax.ShapeDtypeStruct((n_col, tile, width), bf16),
            jax.ShapeDtypeStruct((n_row, tile, width), bf16),
            jax.ShapeDtypeStruct((n_row,) + edge_weight.shape[3:], edge_weight.dtype),
        ),
        in_specs=[vmem] * 3,
        out_specs=(hbm,) * 3,
        scratch_shapes=[
            pltpu.SemaphoreType.DMA((copies,)),
            pltpu.SemaphoreType.DMA((copies,)),
            pltpu.SemaphoreType.DMA((3,)),
        ],
        compiler_params=pltpu.CompilerParams(collective_id=0, has_side_effects=True),
        name="exchange",
    )(queries, normalized, edge_weight[0, 0])
    key_value = jnp.dot(
        norm_group.reshape(n_row * tile, width), w_keyvalue, preferred_element_type=f32
    ).astype(bf16)
    table = jnp.pad(bias_table.T, ((0, 0), (0, tile - bias_table.shape[0])))
    partial_out, partial_level = pl.pallas_call(
        functools.partial(attend, slot_cap, dim ** (-0.5)),
        out_shape=(
            jax.ShapeDtypeStruct((n_col, tile, width), bf16),
            jax.ShapeDtypeStruct((n_col, heads, tile), f32),
        ),
        in_specs=[smem, smem] + [vmem] * 5,
        out_specs=(vmem, vmem),
        scratch_shapes=[pltpu.VMEM((n_col, heads, tile, tile), f32)] * 2
        + [pltpu.VMEM((n_col, heads, tile, dim), f32)],
        compiler_params=pltpu.CompilerParams(vmem_limit_bytes=VMEM_LIMIT),
        name="attend",
    )(
        pair_blocks.reshape(2, slots),
        edge_slope,
        table,
        query_range,
        key_value.reshape(n_row, tile, 2 * width),
        edge_values.reshape(slots, tile, tile),
        bucket_ids.reshape(slots, tile, tile),
    )
    attention = pl.pallas_call(
        functools.partial(combine, n_chip),
        out_shape=jax.ShapeDtypeStruct((tile, width), bf16),
        in_specs=[vmem] * 2,
        out_specs=vmem,
        scratch_shapes=[
            pltpu.VMEM((n_chip, tile, width), bf16),
            pltpu.VMEM((n_chip, heads, tile), f32),
        ]
        * 3
        + [pltpu.SemaphoreType.DMA((4 * n_chip,))] * 2,
        compiler_params=pltpu.CompilerParams(
            collective_id=1, has_side_effects=True, vmem_limit_bytes=VMEM_LIMIT
        ),
        name="combine",
    )(partial_out, partial_level)
    update = jnp.dot(attention, w_out, preferred_element_type=f32)
    return (node_features.astype(f32) + update).astype(bf16)


def solution(mesh):
    return jax.shard_map(
        functools.partial(local, mesh.shape["row"], mesh.shape["col"]),
        mesh=mesh,
        in_specs=(
            P(("row", "col"), None),
            P(),
            P(),
            P(),
            P(),
            P(),
            P(),
            P("row", "col", None, None),
            P("row", "col", None, None, None),
            P("row", "col", None, None, None, None),
        ),
        out_specs=P(("row", "col"), None),
        check_vma=False,
    )
```

```python
import functools

import jax
import jax.numpy as jnp
from jax import lax
from jax.experimental import pallas as pl
from jax.experimental.pallas import tpu as pltpu
from jax.sharding import PartitionSpec as P

EPSILON = 1e-05
LOW_FLOOR = -1e30
CORES = 2
MESH = pl.DeviceIdType.MESH
LANES = 128
VMEM_LIMIT = 60 * 2**20


def normalize(features, gain_vec):
    as_float = features.astype(jnp.float32)
    centered = as_float - jnp.mean(as_float, axis=-1, keepdims=True)
    variance = jnp.mean(centered * centered, axis=-1, keepdims=True)
    return (centered * lax.rsqrt(variance + EPSILON) * gain_vec).astype(jnp.bfloat16)


def greet(partners):
    barrier = pltpu.get_barrier_semaphore()
    for partner in partners:
        pl.semaphore_signal(barrier, inc=1, device_id=partner, device_id_type=MESH)
    pl.semaphore_wait(barrier, len(partners))


def exchange(
    n_row, n_chip, q_in, n_in, e_in, w_in, q_out, k_out, v_out, e_out,
    n_buf, w_buf, send_sem, recv_sem, chip_sem, line_sem, own_sem,
):
    row, col = lax.axis_index("row"), lax.axis_index("col")
    chip, core = col // CORES, col % CORES
    sibling = (row, chip * CORES + (1 - core))
    chips = [(row, ((chip + k) % n_chip) * CORES + core) for k in range(1, n_chip)]
    rows = [((row + k) % n_row, col) for k in range(1, n_row)]
    width = n_in.shape[1]
    greet(chips + [sibling] + rows)

    def remote(src, dst, send, recv, where):
        return pltpu.make_async_remote_copy(
            src_ref=src,
            dst_ref=dst,
            send_sem=send,
            recv_sem=recv,
            device_id=where,
            device_id_type=MESH,
        )

    def hop(step, way):
        origin = chip - way * step
        spot = origin * CORES + core
        copy = remote(
            q_in if step == 0 else q_out.at[spot],
            q_out.at[spot],
            line_sem.at[step, (way + 1) // 2],
            chip_sem.at[origin],
            (row, (chip + way) * CORES + core),
        )
        onward = (chip + way >= 0) & (chip + way < n_chip)
        return copy, onward, (origin >= 0) & (origin < n_chip), spot, origin

    for way in (1, -1):
        copy, onward, _, _, _ = hop(0, way)

        @pl.when(onward)
        def _():
            copy.start()

    n_send = [
        remote(n_in, n_buf.at[k], send_sem.at[k], recv_sem.at[k], where)
        for k, where in enumerate(rows, 1)
    ]
    for copy in n_send:
        copy.start()
    e_send = [
        remote(
            e_in.at[where[0]], e_out.at[row], send_sem.at[n_row + k], recv_sem.at[n_row + k], where
        )
        for k, where in enumerate(rows, 1)
    ]
    for copy in e_send:
        copy.start()
    pair_send = remote(q_in, q_out.at[col], send_sem.at[0], recv_sem.at[0], sibling)
    pair_send.start()
    own = [
        pltpu.make_async_copy(q_in, q_out.at[col], own_sem.at[0]),
        pltpu.make_async_copy(e_in.at[row], e_out.at[row], own_sem.at[1]),
    ]
    weights = pltpu.make_async_copy(w_in, w_buf, own_sem.at[2])
    weights.start()
    for copy in own:
        copy.start()

    def project(rows_ref, spot):
        chunk = 2 * LANES
        hidden = rows_ref[...]

        @pl.loop(0, width // chunk)
        def _(step):
            left = pl.multiple_of(step * chunk, chunk)
            k_out[spot, :, pl.ds(left, chunk)] = jnp.dot(
                hidden, w_buf[:, pl.ds(left, chunk)], preferred_element_type=jnp.float32
            ).astype(k_out.dtype)
            right = pl.multiple_of(width + left, chunk)
            value = jnp.dot(hidden, w_buf[:, pl.ds(right, chunk)], preferred_element_type=jnp.float32)
            v_out[spot, pl.ds(left, chunk), :] = value.T.astype(v_out.dtype)

    weights.wait()
    project(n_in, row)

    def pass_on(step):
        for way in (1, -1):
            copy, onward, real, spot, origin = hop(step, way)

            @pl.when(real)
            def _():
                arrived = q_out.at[spot]
                copy.wait_recv()
                remote(
                    arrived,
                    arrived,
                    send_sem.at[2 * n_row + origin],
                    recv_sem.at[2 * n_row + origin],
                    sibling,
                ).start()

            if step < n_chip - 1:

                @pl.when(real & onward)
                def _():
                    hop(step, way)[0].start()

    for k in range(1, max(n_row, n_chip)):
        if k < n_chip:
            pass_on(k)
        if k < n_row:
            n_send[k - 1].wait_recv()
            project(n_buf.at[k], (row + n_row - k) % n_row)

    for way in (1, -1):
        for step in range(n_chip - 1):
            copy, onward, real, _, _ = hop(step, way)

            @pl.when(real & onward)
            def _():
                copy.wait_send()

        for step in range(1, n_chip):
            _, _, real, spot, origin = hop(step, way)

            @pl.when(real)
            def _():
                remote(
                    q_out.at[spot],
                    q_out.at[spot],
                    send_sem.at[2 * n_row + origin],
                    recv_sem.at[2 * n_row + origin],
                    sibling,
                ).wait()

    for copy in n_send:
        copy.wait_send()
    for copy in e_send + [pair_send]:
        copy.wait()
    for copy in own:
        copy.wait()


def attend(
    slot_cap, scale, pairs, slope, bias_ref, q_ref, k_ref, v_ref, e_ref, b_ref, o_ref, l_ref,
    m_acc, s_acc, o_acc, table, scores,
):
    query_count, heads, tile = l_ref.shape
    dim = q_ref.shape[2] // heads
    buckets_in = bias_ref.shape[0]
    m_acc[...] = jnp.full(m_acc.shape, LOW_FLOOR, jnp.float32)
    s_acc[...] = jnp.zeros(s_acc.shape, jnp.float32)
    o_acc[...] = jnp.zeros(o_acc.shape, jnp.float32)
    scores[0] = jnp.zeros(scores.shape[1:], jnp.float32)
    scores[0, :buckets_in, :heads] = bias_ref[...]
    table[...] = scores[0].T[:heads]

    def slot_step(slot, carry):
        query = pairs[0, slot]

        @pl.when(query >= 0)
        def _():
            key = pairs[1, slot] + slot // slot_cap
            buckets = b_ref[slot].T
            edges = e_ref[slot].astype(jnp.float32).T
            tops = []
            for h in range(heads):
                cols = slice(h * dim, (h + 1) * dim)
                score = lax.dot_general(
                    k_ref[key, :, cols],
                    q_ref[query, :, cols],
                    (((1,), (1,)), ((), ())),
                    preferred_element_type=jnp.float32,
                )
                entries = jnp.broadcast_to(table[h : h + 1, :], (tile, tile))
                bias = jnp.take_along_axis(entries, buckets, axis=1, mode="promise_in_bounds")
                score = score * scale + bias + slope[h] * edges
                scores[h] = score
                tops.append(jnp.max(score, axis=0, keepdims=True))
            old_max = m_acc[query]
            new_max = jnp.maximum(old_max, jnp.concatenate(tops, axis=0))
            keep = jnp.exp(old_max - new_max)
            m_acc[query] = new_max
            sums = []
            for h in range(heads):
                probs = jnp.exp(scores[h] - new_max[h : h + 1]).astype(jnp.bfloat16)
                sums.append(jnp.sum(probs.astype(jnp.float32), axis=0, keepdims=True))
                scores[h] = jnp.dot(
                    v_ref[key, h * dim : (h + 1) * dim, :], probs, preferred_element_type=jnp.float32
                )
            s_acc[query] = s_acc[query] * keep + jnp.concatenate(sums, axis=0)
            for h in range(heads):
                o_acc[query, h] = o_acc[query, h] * keep[h : h + 1] + scores[h]

        return carry

    lax.fori_loop(0, pairs.shape[1], slot_step, 0)

    def finish(query, carry):
        total = s_acc[query]
        live = total > 0.0
        safe = jnp.where(live, total, 1.0)
        l_ref[query] = jnp.where(live, m_acc[query] + jnp.log(safe), LOW_FLOOR)
        share = 1.0 / safe
        for h in range(heads):
            o_ref[query, h * dim : (h + 1) * dim, :] = (o_acc[query, h] * share[h : h + 1]).astype(
                o_ref.dtype
            )
        return carry

    lax.fori_loop(0, query_count, finish, 0)


def blend(levels, parts, heads):
    top = functools.reduce(jnp.maximum, levels)
    shares = [jnp.exp(level - top) for level in levels]
    total = functools.reduce(jnp.add, shares)
    weights = [share / total for share in shares]
    dim = parts[0].shape[0] // heads
    out = []
    for h in range(heads):
        rows = slice(h * dim, (h + 1) * dim)
        terms = [w[h : h + 1] * part[rows].astype(jnp.float32) for w, part in zip(weights, parts)]
        out.append(functools.reduce(jnp.add, terms))
    return out, top + jnp.log(total)


def combine(
    n_chip, o_ref, l_ref, a_ref, sib_o, sib_l, mix_o, mix_l, got_o, got_l, send_sem, recv_sem
):
    row, col = lax.axis_index("row"), lax.axis_index("col")
    chip, core = col // CORES, col % CORES
    heads = l_ref.shape[1]
    dim = o_ref.shape[1] // heads
    sibling = (row, chip * CORES + (1 - core))
    chips = [(row, ((chip + k) % n_chip) * CORES + core) for k in range(1, n_chip)]
    greet(chips + [sibling])

    def send(spot, src, dst, where):
        copy = pltpu.make_async_remote_copy(
            src_ref=src,
            dst_ref=dst,
            send_sem=send_sem.at[spot],
            recv_sem=recv_sem.at[spot],
            device_id=where,
            device_id_type=MESH,
        )
        copy.start()
        return copy

    order = list(range(1, n_chip)) + [0]
    to_sibling = {}
    for k in order:
        theirs = ((chip + k) % n_chip) * CORES + (1 - core)
        to_sibling[k] = [
            send(4 * k, l_ref.at[theirs], sib_l.at[k], sibling),
            send(4 * k + 1, o_ref.at[theirs], sib_o.at[k], sibling),
        ]
    over = []

    def push(k):
        over.append(send(4 * k + 2, mix_l.at[k], got_l.at[k], chips[k - 1]))
        over.append(send(4 * k + 3, mix_o.at[k], got_o.at[k], chips[k - 1]))

    for k in range(1, n_chip):
        for copy in to_sibling[k]:
            copy.wait_recv()
        mine = ((chip + k) % n_chip) * CORES + core
        out, level = blend([l_ref[mine], sib_l[k]], [o_ref[mine], sib_o[k]], heads)
        for h in range(heads):
            mix_o[k, h * dim : (h + 1) * dim, :] = out[h].astype(mix_o.dtype)
        mix_l[k] = level
        push(k)
    for copy in to_sibling[0]:
        copy.wait_recv()
    for copy in over:
        copy.wait_recv()
    levels = [l_ref[col], sib_l[0]] + [got_l[k] for k in range(1, n_chip)]
    parts = [o_ref[col], sib_o[0]] + [got_o[k] for k in range(1, n_chip)]
    out, _ = blend(levels, parts, heads)
    for h in range(heads):
        a_ref[h * dim : (h + 1) * dim, :] = out[h].astype(a_ref.dtype)
    for copies in to_sibling.values():
        for copy in copies:
            copy.wait_send()
    for copy in over:
        copy.wait_send()


def local(
    n_row,
    n_col,
    node_features,
    norm_gain,
    w_query,
    w_keyvalue,
    w_out,
    bias_table,
    edge_slope,
    pair_blocks,
    bucket_ids,
    edge_weight,
):
    tile, width = node_features.shape
    heads = edge_slope.shape[0]
    dim = width // heads
    n_chip = n_col // CORES
    slot_cap = edge_weight.shape[3]
    slots = n_row * slot_cap
    bf16, f32 = jnp.bfloat16, jnp.float32
    vmem = pl.BlockSpec(memory_space=pltpu.VMEM)
    smem = pl.BlockSpec(memory_space=pltpu.SMEM)
    hbm = pl.BlockSpec(memory_space=pl.ANY)

    normalized = normalize(node_features, norm_gain)
    queries = jnp.dot(normalized, w_query, preferred_element_type=f32).astype(bf16)
    copies = 2 * n_row + n_chip
    query_range, keys, values, edge_values = pl.pallas_call(
        functools.partial(exchange, n_row, n_chip),
        out_shape=(
            jax.ShapeDtypeStruct((n_col, tile, width), bf16),
            jax.ShapeDtypeStruct((n_row, tile, width), bf16),
            jax.ShapeDtypeStruct((n_row, width, tile), bf16),
            jax.ShapeDtypeStruct((n_row,) + edge_weight.shape[3:], edge_weight.dtype),
        ),
        in_specs=[vmem] * 3 + [hbm],
        out_specs=(hbm, vmem, vmem, hbm),
        scratch_shapes=[
            pltpu.VMEM((n_row, tile, width), bf16),
            pltpu.VMEM(w_keyvalue.shape, bf16),
            pltpu.SemaphoreType.DMA((copies,)),
            pltpu.SemaphoreType.DMA((copies,)),
            pltpu.SemaphoreType.DMA((n_chip,)),
            pltpu.SemaphoreType.DMA((n_chip, 2)),
            pltpu.SemaphoreType.DMA((3,)),
        ],
        compiler_params=pltpu.CompilerParams(
            collective_id=0, has_side_effects=True, vmem_limit_bytes=VMEM_LIMIT
        ),
        name="exchange",
    )(queries, normalized, edge_weight[0, 0], w_keyvalue)
    partial_out, partial_level = pl.pallas_call(
        functools.partial(attend, slot_cap, dim ** (-0.5)),
        out_shape=(
            jax.ShapeDtypeStruct((n_col, width, tile), bf16),
            jax.ShapeDtypeStruct((n_col, heads, tile), f32),
        ),
        in_specs=[smem, smem] + [vmem] * 6,
        out_specs=(vmem, vmem),
        scratch_shapes=[
            pltpu.VMEM((n_col, heads, tile), f32),
            pltpu.VMEM((n_col, heads, tile), f32),
            pltpu.VMEM((n_col, heads, dim, tile), f32),
            pltpu.VMEM((heads, tile), f32),
            pltpu.VMEM((heads, tile, tile), f32),
        ],
        compiler_params=pltpu.CompilerParams(vmem_limit_bytes=VMEM_LIMIT),
        name="attend",
    )(
        pair_blocks.reshape(2, slots),
        edge_slope,
        bias_table,
        query_range,
        keys,
        values,
        edge_values.reshape(slots, tile, tile),
        bucket_ids.reshape(slots, tile, tile),
    )
    attention = pl.pallas_call(
        functools.partial(combine, n_chip),
        out_shape=jax.ShapeDtypeStruct((width, tile), bf16),
        in_specs=[vmem] * 2,
        out_specs=vmem,
        scratch_shapes=[
            pltpu.VMEM((n_chip, width, tile), bf16),
            pltpu.VMEM((n_chip, heads, tile), f32),
        ]
        * 3
        + [pltpu.SemaphoreType.DMA((4 * n_chip,))] * 2,
        compiler_params=pltpu.CompilerParams(
            collective_id=1, has_side_effects=True, vmem_limit_bytes=VMEM_LIMIT
        ),
        name="combine",
    )(partial_out, partial_level)
    update = lax.dot_general(
        attention, w_out, (((0,), (0,)), ((), ())), preferred_element_type=f32
    )
    return (node_features.astype(f32) + update).astype(bf16)


def solution(mesh):
    return jax.shard_map(
        functools.partial(local, mesh.shape["row"], mesh.shape["col"]),
        mesh=mesh,
        in_specs=(
            P(("row", "col"), None),
            P(),
            P(),
            P(),
            P(),
            P(),
            P(),
            P("row", "col", None, None),
            P("row", "col", None, None, None),
            P("row", "col", None, None, None, None),
        ),
        out_specs=P(("row", "col"), None),
        check_vma=False,
    )
```

```python
import functools

import jax
import jax.numpy as jnp
from jax import lax
from jax.experimental import pallas as pl
from jax.experimental.pallas import tpu as pltpu
from jax.sharding import PartitionSpec as P

EPSILON = 1e-05
LOW_FLOOR = -1e30
CORES = 2
MESH = pl.DeviceIdType.MESH
LANES = 128
VMEM_LIMIT = 60 * 2**20


def normalize(features, gain_vec):
    as_float = features.astype(jnp.float32)
    centered = as_float - jnp.mean(as_float, axis=-1, keepdims=True)
    variance = jnp.mean(centered * centered, axis=-1, keepdims=True)
    return (centered * lax.rsqrt(variance + EPSILON) * gain_vec).astype(jnp.bfloat16)


def greet(partners):
    barrier = pltpu.get_barrier_semaphore()
    for partner in partners:
        pl.semaphore_signal(barrier, inc=1, device_id=partner, device_id_type=MESH)
    pl.semaphore_wait(barrier, len(partners))


def exchange(
    n_row, n_chip, x_in, gain_in, e_in, wq_in, w_in, q_out, k_out, v_out, e_out,
    q_in, n_in, n_buf, wq_buf, w_buf, send_sem, recv_sem, chip_sem, line_sem, own_sem,
):
    row, col = lax.axis_index("row"), lax.axis_index("col")
    chip, core = col // CORES, col % CORES
    sibling = (row, chip * CORES + (1 - core))
    chips = [(row, ((chip + k) % n_chip) * CORES + core) for k in range(1, n_chip)]
    rows = [((row + k) % n_row, col) for k in range(1, n_row)]
    width = n_in.shape[1]
    query_weights = pltpu.make_async_copy(wq_in, wq_buf, own_sem.at[3])
    weights = pltpu.make_async_copy(w_in, w_buf, own_sem.at[2])
    query_weights.start()
    greet(chips + [sibling] + rows)

    def remote(src, dst, send, recv, where):
        return pltpu.make_async_remote_copy(
            src_ref=src,
            dst_ref=dst,
            send_sem=send,
            recv_sem=recv,
            device_id=where,
            device_id_type=MESH,
        )

    def hop(step, way):
        origin = chip - way * step
        spot = origin * CORES + core
        copy = remote(
            q_in if step == 0 else q_out.at[spot],
            q_out.at[spot],
            line_sem.at[step, (way + 1) // 2],
            chip_sem.at[origin],
            (row, (chip + way) * CORES + core),
        )
        onward = (chip + way >= 0) & (chip + way < n_chip)
        return copy, onward, (origin >= 0) & (origin < n_chip), spot, origin

    weights.start()
    e_send = [
        remote(
            e_in.at[where[0]], e_out.at[row], send_sem.at[n_row + k], recv_sem.at[n_row + k], where
        )
        for k, where in enumerate(rows, 1)
    ]
    n_in[...] = normalize(x_in[...], gain_in[...])
    query_weights.wait()
    n_send = [
        remote(n_in, n_buf.at[k], send_sem.at[k], recv_sem.at[k], where)
        for k, where in enumerate(rows, 1)
    ]
    chunk = 2 * LANES

    @pl.loop(0, width // chunk)
    def _(step):
        left = pl.multiple_of(step * chunk, chunk)
        q_in[:, pl.ds(left, chunk)] = jnp.dot(
            n_in[...], wq_buf[:, pl.ds(left, chunk)], preferred_element_type=jnp.float32
        ).astype(q_in.dtype)

    for copy in n_send:
        copy.start()
    for way in (1, -1):
        copy, onward, _, _, _ = hop(0, way)

        @pl.when(onward)
        def _():
            copy.start()

    for copy in e_send:
        copy.start()
    pair_send = remote(q_in, q_out.at[col], send_sem.at[0], recv_sem.at[0], sibling)
    pair_send.start()
    own = [
        pltpu.make_async_copy(q_in, q_out.at[col], own_sem.at[0]),
        pltpu.make_async_copy(e_in.at[row], e_out.at[row], own_sem.at[1]),
    ]
    for copy in own:
        copy.start()

    def project(rows_ref, spot):
        hidden = rows_ref[...]

        @pl.loop(0, width // chunk)
        def _(step):
            left = pl.multiple_of(step * chunk, chunk)
            k_out[spot, :, pl.ds(left, chunk)] = jnp.dot(
                hidden, w_buf[:, pl.ds(left, chunk)], preferred_element_type=jnp.float32
            ).astype(k_out.dtype)
            right = pl.multiple_of(width + left, chunk)
            value = jnp.dot(hidden, w_buf[:, pl.ds(right, chunk)], preferred_element_type=jnp.float32)
            v_out[spot, pl.ds(left, chunk), :] = value.T.astype(v_out.dtype)

    weights.wait()
    project(n_in, row)

    def pass_on(step):
        for way in (1, -1):
            copy, onward, real, spot, origin = hop(step, way)

            @pl.when(real)
            def _():
                arrived = q_out.at[spot]
                copy.wait_recv()
                remote(
                    arrived,
                    arrived,
                    send_sem.at[2 * n_row + origin],
                    recv_sem.at[2 * n_row + origin],
                    sibling,
                ).start()

            if step < n_chip - 1:

                @pl.when(real & onward)
                def _():
                    hop(step, way)[0].start()

    for k in range(1, max(n_row, n_chip)):
        if k < n_chip:
            pass_on(k)
        if k < n_row:
            n_send[k - 1].wait_recv()
            project(n_buf.at[k], (row + n_row - k) % n_row)

    for way in (1, -1):
        for step in range(n_chip - 1):
            copy, onward, real, _, _ = hop(step, way)

            @pl.when(real & onward)
            def _():
                copy.wait_send()

        for step in range(1, n_chip):
            _, _, real, spot, origin = hop(step, way)

            @pl.when(real)
            def _():
                remote(
                    q_out.at[spot],
                    q_out.at[spot],
                    send_sem.at[2 * n_row + origin],
                    recv_sem.at[2 * n_row + origin],
                    sibling,
                ).wait()

    for copy in n_send:
        copy.wait_send()
    for copy in e_send + [pair_send]:
        copy.wait()
    for copy in own:
        copy.wait()


def attend(
    slot_cap, scale, pairs, slope, bias_ref, q_ref, k_ref, v_ref, e_ref, b_ref, o_ref, l_ref,
    m_acc, s_acc, o_acc, table, scores,
):
    query_count, heads, tile = l_ref.shape
    dim = q_ref.shape[2] // heads
    buckets_in = bias_ref.shape[1]
    m_acc[...] = jnp.full(m_acc.shape, LOW_FLOOR, jnp.float32)
    s_acc[...] = jnp.zeros(s_acc.shape, jnp.float32)
    o_acc[...] = jnp.zeros(o_acc.shape, jnp.float32)
    table[...] = jnp.zeros(table.shape, jnp.float32)
    table[:, :buckets_in] = bias_ref[...]

    def slot_step(slot, carry):
        query = pairs[0, slot]

        @pl.when(query >= 0)
        def _():
            key = pairs[1, slot] + slot // slot_cap
            buckets = b_ref[slot].T
            edges = e_ref[slot].astype(jnp.float32).T
            tops = []
            for h in range(heads):
                cols = slice(h * dim, (h + 1) * dim)
                score = lax.dot_general(
                    k_ref[key, :, cols],
                    q_ref[query, :, cols],
                    (((1,), (1,)), ((), ())),
                    preferred_element_type=jnp.float32,
                )
                entries = jnp.broadcast_to(table[h : h + 1, :], (tile, tile))
                bias = jnp.take_along_axis(entries, buckets, axis=1, mode="promise_in_bounds")
                score = score * scale + bias + slope[h] * edges
                scores[h] = score
                tops.append(jnp.max(score, axis=0, keepdims=True))
            old_max = m_acc[query]
            new_max = jnp.maximum(old_max, jnp.concatenate(tops, axis=0))
            keep = jnp.exp(old_max - new_max)
            m_acc[query] = new_max
            sums = []
            for h in range(heads):
                probs = jnp.exp(scores[h] - new_max[h : h + 1]).astype(jnp.bfloat16)
                sums.append(jnp.sum(probs.astype(jnp.float32), axis=0, keepdims=True))
                scores[h] = jnp.dot(
                    v_ref[key, h * dim : (h + 1) * dim, :], probs, preferred_element_type=jnp.float32
                )
            s_acc[query] = s_acc[query] * keep + jnp.concatenate(sums, axis=0)
            for h in range(heads):
                o_acc[query, h] = o_acc[query, h] * keep[h : h + 1] + scores[h]

        return carry

    lax.fori_loop(0, pairs.shape[1], slot_step, 0)

    def finish(query, carry):
        total = s_acc[query]
        live = total > 0.0
        safe = jnp.where(live, total, 1.0)
        l_ref[query] = jnp.where(live, m_acc[query] + jnp.log(safe), LOW_FLOOR)
        share = 1.0 / safe
        for h in range(heads):
            o_ref[query, h * dim : (h + 1) * dim, :] = (o_acc[query, h] * share[h : h + 1]).astype(
                o_ref.dtype
            )
        return carry

    lax.fori_loop(0, query_count, finish, 0)


def blend(levels, parts, heads):
    top = functools.reduce(jnp.maximum, levels)
    shares = [jnp.exp(level - top) for level in levels]
    total = functools.reduce(jnp.add, shares)
    weights = [share / total for share in shares]
    dim = parts[0].shape[0] // heads
    out = []
    for h in range(heads):
        rows = slice(h * dim, (h + 1) * dim)
        terms = [w[h : h + 1] * part[rows].astype(jnp.float32) for w, part in zip(weights, parts)]
        out.append(functools.reduce(jnp.add, terms))
    return out, top + jnp.log(total)


def partner(chip, k, n_chip):
    if n_chip & (n_chip - 1):
        return (chip + k) % n_chip
    bits = [1 << b for b in range(n_chip.bit_length() - 1)]
    return sum(((chip // bit + k // bit) % 2) * bit for bit in bits)


def combine(
    n_chip, o_ref, l_ref, a_ref, sib_o, sib_l, mix_o, mix_l, got_o, got_l, send_sem, recv_sem
):
    row, col = lax.axis_index("row"), lax.axis_index("col")
    chip, core = col // CORES, col % CORES
    heads = l_ref.shape[1]
    dim = o_ref.shape[1] // heads
    sibling = (row, chip * CORES + (1 - core))
    chips = [(row, partner(chip, k, n_chip) * CORES + core) for k in range(1, n_chip)]
    greet(chips + [sibling])

    def send(spot, src, dst, where):
        copy = pltpu.make_async_remote_copy(
            src_ref=src,
            dst_ref=dst,
            send_sem=send_sem.at[spot],
            recv_sem=recv_sem.at[spot],
            device_id=where,
            device_id_type=MESH,
        )
        copy.start()
        return copy

    half = n_chip // 2
    far = list(range(half, n_chip)) + list(range(1, half))
    order = far + [0]
    to_sibling = {}
    for k in order:
        theirs = partner(chip, k, n_chip) * CORES + (1 - core)
        to_sibling[k] = [
            send(4 * k, l_ref.at[theirs], sib_l.at[k], sibling),
            send(4 * k + 1, o_ref.at[theirs], sib_o.at[k], sibling),
        ]
    over = []

    def push(k):
        over.append(send(4 * k + 2, mix_l.at[k], got_l.at[k], chips[k - 1]))
        over.append(send(4 * k + 3, mix_o.at[k], got_o.at[k], chips[k - 1]))

    for k in far:
        for copy in to_sibling[k]:
            copy.wait_recv()
        mine = partner(chip, k, n_chip) * CORES + core
        out, level = blend([l_ref[mine], sib_l[k]], [o_ref[mine], sib_o[k]], heads)
        for h in range(heads):
            mix_o[k, h * dim : (h + 1) * dim, :] = out[h].astype(mix_o.dtype)
        mix_l[k] = level
        push(k)
    for copy in to_sibling[0]:
        copy.wait_recv()
    for copy in over:
        copy.wait_recv()
    levels = [l_ref[col], sib_l[0]] + [got_l[k] for k in range(1, n_chip)]
    parts = [o_ref[col], sib_o[0]] + [got_o[k] for k in range(1, n_chip)]
    out, _ = blend(levels, parts, heads)
    for h in range(heads):
        a_ref[h * dim : (h + 1) * dim, :] = out[h].astype(a_ref.dtype)
    for copies in to_sibling.values():
        for copy in copies:
            copy.wait_send()
    for copy in over:
        copy.wait_send()


def local(
    n_row,
    n_col,
    node_features,
    norm_gain,
    w_query,
    w_keyvalue,
    w_out,
    bias_table,
    edge_slope,
    pair_blocks,
    bucket_ids,
    edge_weight,
):
    tile, width = node_features.shape
    heads = edge_slope.shape[0]
    dim = width // heads
    n_chip = n_col // CORES
    slot_cap = edge_weight.shape[3]
    slots = n_row * slot_cap
    bf16, f32 = jnp.bfloat16, jnp.float32
    vmem = pl.BlockSpec(memory_space=pltpu.VMEM)
    smem = pl.BlockSpec(memory_space=pltpu.SMEM)
    hbm = pl.BlockSpec(memory_space=pl.ANY)

    copies = 2 * n_row + n_chip
    query_range, keys, values, edge_values = pl.pallas_call(
        functools.partial(exchange, n_row, n_chip),
        out_shape=(
            jax.ShapeDtypeStruct((n_col, tile, width), bf16),
            jax.ShapeDtypeStruct((n_row, tile, width), bf16),
            jax.ShapeDtypeStruct((n_row, width, tile), bf16),
            jax.ShapeDtypeStruct((n_row,) + edge_weight.shape[3:], edge_weight.dtype),
        ),
        in_specs=[vmem] * 3 + [hbm] * 2,
        out_specs=(hbm, vmem, vmem, hbm),
        scratch_shapes=[
            pltpu.VMEM((tile, width), bf16),
            pltpu.VMEM((tile, width), bf16),
            pltpu.VMEM((n_row, tile, width), bf16),
            pltpu.VMEM(w_query.shape, bf16),
            pltpu.VMEM(w_keyvalue.shape, bf16),
            pltpu.SemaphoreType.DMA((copies,)),
            pltpu.SemaphoreType.DMA((copies,)),
            pltpu.SemaphoreType.DMA((n_chip,)),
            pltpu.SemaphoreType.DMA((n_chip, 2)),
            pltpu.SemaphoreType.DMA((4,)),
        ],
        compiler_params=pltpu.CompilerParams(
            collective_id=0, has_side_effects=True, vmem_limit_bytes=VMEM_LIMIT
        ),
        name="exchange",
    )(node_features, norm_gain[None], edge_weight[0, 0], w_query, w_keyvalue)
    partial_out, partial_level = pl.pallas_call(
        functools.partial(attend, slot_cap, dim ** (-0.5)),
        out_shape=(
            jax.ShapeDtypeStruct((n_col, width, tile), bf16),
            jax.ShapeDtypeStruct((n_col, heads, tile), f32),
        ),
        in_specs=[smem, smem] + [vmem] * 6,
        out_specs=(vmem, vmem),
        scratch_shapes=[
            pltpu.VMEM((n_col, heads, tile), f32),
            pltpu.VMEM((n_col, heads, tile), f32),
            pltpu.VMEM((n_col, heads, dim, tile), f32),
            pltpu.VMEM((heads, tile), f32),
            pltpu.VMEM((heads, tile, tile), f32),
        ],
        compiler_params=pltpu.CompilerParams(vmem_limit_bytes=VMEM_LIMIT),
        name="attend",
    )(
        pair_blocks.reshape(2, slots),
        edge_slope,
        bias_table.T,
        query_range,
        keys,
        values,
        edge_values.reshape(slots, tile, tile),
        bucket_ids.reshape(slots, tile, tile),
    )
    attention = pl.pallas_call(
        functools.partial(combine, n_chip),
        out_shape=jax.ShapeDtypeStruct((width, tile), bf16),
        in_specs=[vmem] * 2,
        out_specs=vmem,
        scratch_shapes=[
            pltpu.VMEM((n_chip, width, tile), bf16),
            pltpu.VMEM((n_chip, heads, tile), f32),
        ]
        * 3
        + [pltpu.SemaphoreType.DMA((4 * n_chip,))] * 2,
        compiler_params=pltpu.CompilerParams(
            collective_id=1, has_side_effects=True, vmem_limit_bytes=VMEM_LIMIT
        ),
        name="combine",
    )(partial_out, partial_level)
    update = lax.dot_general(
        attention, w_out, (((0,), (0,)), ((), ())), preferred_element_type=f32
    )
    return (node_features.astype(f32) + update).astype(bf16)


def solution(mesh):
    return jax.shard_map(
        functools.partial(local, mesh.shape["row"], mesh.shape["col"]),
        mesh=mesh,
        in_specs=(
            P(("row", "col"), None),
            P(),
            P(),
            P(),
            P(),
            P(),
            P(),
            P("row", "col", None, None),
            P("row", "col", None, None, None),
            P("row", "col", None, None, None, None),
        ),
        out_specs=P(("row", "col"), None),
        check_vma=False,
    )
```

```python
import functools

import jax
import jax.numpy as jnp
from jax import lax
from jax.experimental import pallas as pl
from jax.experimental.pallas import tpu as pltpu
from jax.sharding import PartitionSpec as P

EPSILON = 1e-05
LOW_FLOOR = -1e30
CORES = 2
MESH = pl.DeviceIdType.MESH
LANES = 128
VMEM_LIMIT = 60 * 2**20


def normalize(features, gain_vec):
    as_float = features.astype(jnp.float32)
    centered = as_float - jnp.mean(as_float, axis=-1, keepdims=True)
    variance = jnp.mean(centered * centered, axis=-1, keepdims=True)
    return (centered * lax.rsqrt(variance + EPSILON) * gain_vec).astype(jnp.bfloat16)


def greet(partners):
    barrier = pltpu.get_barrier_semaphore()
    for partner in partners:
        pl.semaphore_signal(barrier, inc=1, device_id=partner, device_id_type=MESH)
    pl.semaphore_wait(barrier, len(partners))


def exchange(
    n_row, n_chip, x_in, gain_in, e_in, wq_in, w_in, q_out, k_out, v_out, e_out,
    q_in, n_in, n_buf, wq_buf, w_buf, send_sem, recv_sem, chip_sem, line_sem, own_sem,
):
    row, col = lax.axis_index("row"), lax.axis_index("col")
    chip, core = col // CORES, col % CORES
    sibling = (row, chip * CORES + (1 - core))
    chips = [(row, ((chip + k) % n_chip) * CORES + core) for k in range(1, n_chip)]
    rows = [((row + k) % n_row, col) for k in range(1, n_row)]
    width = n_in.shape[1]
    query_weights = pltpu.make_async_copy(wq_in, wq_buf, own_sem.at[3])
    weights = pltpu.make_async_copy(w_in, w_buf, own_sem.at[2])
    query_weights.start()
    greet(chips + [sibling] + rows)

    def remote(src, dst, send, recv, where):
        return pltpu.make_async_remote_copy(
            src_ref=src,
            dst_ref=dst,
            send_sem=send,
            recv_sem=recv,
            device_id=where,
            device_id_type=MESH,
        )

    def hop(step, way):
        origin = chip - way * step
        spot = origin * CORES + core
        copy = remote(
            q_in if step == 0 else q_out.at[spot],
            q_out.at[spot],
            line_sem.at[step, (way + 1) // 2],
            chip_sem.at[origin],
            (row, (chip + way) * CORES + core),
        )
        onward = (chip + way >= 0) & (chip + way < n_chip)
        return copy, onward, (origin >= 0) & (origin < n_chip), spot, origin

    weights.start()
    e_send = [
        remote(
            e_in.at[where[0]], e_out.at[row], send_sem.at[n_row + k], recv_sem.at[n_row + k], where
        )
        for k, where in enumerate(rows, 1)
    ]
    n_in[...] = normalize(x_in[...], gain_in[...])
    query_weights.wait()
    n_send = [
        remote(n_in, n_buf.at[k], send_sem.at[k], recv_sem.at[k], where)
        for k, where in enumerate(rows, 1)
    ]
    chunk = 2 * LANES

    @pl.loop(0, width // chunk)
    def _(step):
        left = pl.multiple_of(step * chunk, chunk)
        q_in[:, pl.ds(left, chunk)] = jnp.dot(
            n_in[...], wq_buf[:, pl.ds(left, chunk)], preferred_element_type=jnp.float32
        ).astype(q_in.dtype)

    for copy in n_send:
        copy.start()
    for way in (1, -1):
        copy, onward, _, _, _ = hop(0, way)

        @pl.when(onward)
        def _():
            copy.start()

    for copy in e_send:
        copy.start()
    pair_send = remote(q_in, q_out.at[col], send_sem.at[0], recv_sem.at[0], sibling)
    pair_send.start()
    own = [
        pltpu.make_async_copy(q_in, q_out.at[col], own_sem.at[0]),
        pltpu.make_async_copy(e_in.at[row], e_out.at[row], own_sem.at[1]),
    ]
    for copy in own:
        copy.start()

    def project(rows_ref, spot):
        hidden = rows_ref[...]

        @pl.loop(0, width // chunk)
        def _(step):
            left = pl.multiple_of(step * chunk, chunk)
            k_out[spot, :, pl.ds(left, chunk)] = jnp.dot(
                hidden, w_buf[:, pl.ds(left, chunk)], preferred_element_type=jnp.float32
            ).astype(k_out.dtype)
            right = pl.multiple_of(width + left, chunk)
            value = jnp.dot(hidden, w_buf[:, pl.ds(right, chunk)], preferred_element_type=jnp.float32)
            v_out[spot, pl.ds(left, chunk), :] = value.T.astype(v_out.dtype)

    weights.wait()
    project(n_in, row)

    def pass_on(step):
        for way in (1, -1):
            copy, onward, real, spot, origin = hop(step, way)

            @pl.when(real)
            def _():
                arrived = q_out.at[spot]
                copy.wait_recv()
                remote(
                    arrived,
                    arrived,
                    send_sem.at[2 * n_row + origin],
                    recv_sem.at[2 * n_row + origin],
                    sibling,
                ).start()

            if step < n_chip - 1:

                @pl.when(real & onward)
                def _():
                    hop(step, way)[0].start()

    for k in range(1, max(n_row, n_chip)):
        if k < n_chip:
            pass_on(k)
        if k < n_row:
            n_send[k - 1].wait_recv()
            project(n_buf.at[k], (row + n_row - k) % n_row)

    for way in (1, -1):
        for step in range(n_chip - 1):
            copy, onward, real, _, _ = hop(step, way)

            @pl.when(real & onward)
            def _():
                copy.wait_send()

        for step in range(1, n_chip):
            _, _, real, spot, origin = hop(step, way)

            @pl.when(real)
            def _():
                remote(
                    q_out.at[spot],
                    q_out.at[spot],
                    send_sem.at[2 * n_row + origin],
                    recv_sem.at[2 * n_row + origin],
                    sibling,
                ).wait()

    for copy in n_send:
        copy.wait_send()
    for copy in e_send + [pair_send]:
        copy.wait()
    for copy in own:
        copy.wait()


def attend(
    slot_cap, scale, pairs, slope, bias_ref, q_in, k_in, v_in, e_in, b_in, o_out, l_ref,
    m_acc, s_acc, o_acc, table, scores, q_ref, k_ref, v_ref, e_ref, b_ref, o_ref,
    whole_sem, slot_sem, out_sem,
):
    whole = [
        pltpu.make_async_copy(src, dst, whole_sem.at[i])
        for i, (src, dst) in enumerate(((q_in, q_ref), (k_in, k_ref), (v_in, v_ref)))
    ]
    for copy in whole:
        copy.start()

    def fetch(slot):
        return (
            pltpu.make_async_copy(b_in.at[slot], b_ref.at[slot], slot_sem.at[0, slot]),
            pltpu.make_async_copy(e_in.at[slot], e_ref.at[slot], slot_sem.at[1, slot]),
        )

    @pl.loop(0, pairs.shape[1])
    def _(slot):
        for copy in fetch(slot):
            copy.start()

    query_count, heads, tile = l_ref.shape
    dim = q_ref.shape[2] // heads
    buckets_in = bias_ref.shape[1]
    m_acc[...] = jnp.full(m_acc.shape, LOW_FLOOR, jnp.float32)
    s_acc[...] = jnp.zeros(s_acc.shape, jnp.float32)
    o_acc[...] = jnp.zeros(o_acc.shape, jnp.float32)
    table[...] = jnp.zeros(table.shape, jnp.float32)
    table[:, :buckets_in] = bias_ref[...]

    for copy in whole:
        copy.wait()

    def slot_step(slot, carry):
        for copy in fetch(slot):
            copy.wait()
        query = pairs[0, slot]

        @pl.when(query >= 0)
        def _():
            key = pairs[1, slot] + slot // slot_cap
            buckets = b_ref[slot].T
            edges = e_ref[slot].astype(jnp.float32).T
            tops = []
            for h in range(heads):
                cols = slice(h * dim, (h + 1) * dim)
                score = lax.dot_general(
                    k_ref[key, :, cols],
                    q_ref[query, :, cols],
                    (((1,), (1,)), ((), ())),
                    preferred_element_type=jnp.float32,
                )
                entries = jnp.broadcast_to(table[h : h + 1, :], (tile, tile))
                bias = jnp.take_along_axis(entries, buckets, axis=1, mode="promise_in_bounds")
                score = score * scale + bias + slope[h] * edges
                scores[h] = score
                tops.append(jnp.max(score, axis=0, keepdims=True))
            old_max = m_acc[query]
            new_max = jnp.maximum(old_max, jnp.concatenate(tops, axis=0))
            keep = jnp.exp(old_max - new_max)
            m_acc[query] = new_max
            sums = []
            for h in range(heads):
                probs = jnp.exp(scores[h] - new_max[h : h + 1]).astype(jnp.bfloat16)
                sums.append(jnp.sum(probs.astype(jnp.float32), axis=0, keepdims=True))
                scores[h] = jnp.dot(
                    v_ref[key, h * dim : (h + 1) * dim, :], probs, preferred_element_type=jnp.float32
                )
            s_acc[query] = s_acc[query] * keep + jnp.concatenate(sums, axis=0)
            for h in range(heads):
                o_acc[query, h] = o_acc[query, h] * keep[h : h + 1] + scores[h]

        return carry

    lax.fori_loop(0, pairs.shape[1], slot_step, 0)

    def finish(query, carry):
        total = s_acc[query]
        live = total > 0.0
        safe = jnp.where(live, total, 1.0)
        l_ref[query] = jnp.where(live, m_acc[query] + jnp.log(safe), LOW_FLOOR)
        share = 1.0 / safe
        for h in range(heads):
            o_ref[query, h * dim : (h + 1) * dim, :] = (o_acc[query, h] * share[h : h + 1]).astype(
                o_ref.dtype
            )
        give(query).start()
        return carry

    def give(query):
        return pltpu.make_async_copy(o_ref.at[query], o_out.at[query], out_sem.at[query])

    lax.fori_loop(0, query_count, finish, 0)

    @pl.loop(0, query_count)
    def _(query):
        give(query).wait()


def blend(levels, parts, heads):
    top = functools.reduce(jnp.maximum, levels)
    shares = [jnp.exp(level - top) for level in levels]
    total = functools.reduce(jnp.add, shares)
    weights = [share / total for share in shares]
    dim = parts[0].shape[0] // heads
    out = []
    for h in range(heads):
        rows = slice(h * dim, (h + 1) * dim)
        terms = [w[h : h + 1] * part[rows].astype(jnp.float32) for w, part in zip(weights, parts)]
        out.append(functools.reduce(jnp.add, terms))
    return out, top + jnp.log(total)


def partner(chip, k, n_chip):
    if n_chip & (n_chip - 1):
        return (chip + k) % n_chip
    bits = [1 << b for b in range(n_chip.bit_length() - 1)]
    return sum(((chip // bit + k // bit) % 2) * bit for bit in bits)


def combine(
    n_chip, o_ref, l_ref, a_ref, sib_o, sib_l, mix_o, mix_l, got_o, got_l, own_o,
    send_sem, recv_sem, own_sem,
):
    row, col = lax.axis_index("row"), lax.axis_index("col")
    chip, core = col // CORES, col % CORES
    heads = l_ref.shape[1]
    dim = o_ref.shape[1] // heads
    sibling = (row, chip * CORES + (1 - core))
    chips = [(row, partner(chip, k, n_chip) * CORES + core) for k in range(1, n_chip)]
    own = [
        pltpu.make_async_copy(
            o_ref.at[partner(chip, k, n_chip) * CORES + core], own_o.at[k], own_sem.at[k]
        )
        for k in range(n_chip)
    ]
    for copy in own:
        copy.start()
    greet(chips + [sibling])

    def send(spot, src, dst, where):
        copy = pltpu.make_async_remote_copy(
            src_ref=src,
            dst_ref=dst,
            send_sem=send_sem.at[spot],
            recv_sem=recv_sem.at[spot],
            device_id=where,
            device_id_type=MESH,
        )
        copy.start()
        return copy

    half = n_chip // 2
    far = list(range(half, n_chip)) + list(range(1, half))
    order = far + [0]
    to_sibling = {}
    for k in order:
        theirs = partner(chip, k, n_chip) * CORES + (1 - core)
        to_sibling[k] = [
            send(4 * k, l_ref.at[theirs], sib_l.at[k], sibling),
            send(4 * k + 1, o_ref.at[theirs], sib_o.at[k], sibling),
        ]
    over = []

    def push(k):
        over.append(send(4 * k + 2, mix_l.at[k], got_l.at[k], chips[k - 1]))
        over.append(send(4 * k + 3, mix_o.at[k], got_o.at[k], chips[k - 1]))

    for k in far:
        for copy in to_sibling[k]:
            copy.wait_recv()
        own[k].wait()
        mine = partner(chip, k, n_chip) * CORES + core
        out, level = blend([l_ref[mine], sib_l[k]], [own_o[k], sib_o[k]], heads)
        for h in range(heads):
            mix_o[k, h * dim : (h + 1) * dim, :] = out[h].astype(mix_o.dtype)
        mix_l[k] = level
        push(k)
    for copy in to_sibling[0]:
        copy.wait_recv()
    for copy in over:
        copy.wait_recv()
    own[0].wait()
    levels = [l_ref[col], sib_l[0]] + [got_l[k] for k in range(1, n_chip)]
    parts = [own_o[0], sib_o[0]] + [got_o[k] for k in range(1, n_chip)]
    out, _ = blend(levels, parts, heads)
    for h in range(heads):
        a_ref[h * dim : (h + 1) * dim, :] = out[h].astype(a_ref.dtype)
    for copies in to_sibling.values():
        for copy in copies:
            copy.wait_send()
    for copy in over:
        copy.wait_send()


def local(
    n_row,
    n_col,
    node_features,
    norm_gain,
    w_query,
    w_keyvalue,
    w_out,
    bias_table,
    edge_slope,
    pair_blocks,
    bucket_ids,
    edge_weight,
):
    tile, width = node_features.shape
    heads = edge_slope.shape[0]
    dim = width // heads
    n_chip = n_col // CORES
    slot_cap = edge_weight.shape[3]
    slots = n_row * slot_cap
    bf16, f32 = jnp.bfloat16, jnp.float32
    vmem = pl.BlockSpec(memory_space=pltpu.VMEM)
    smem = pl.BlockSpec(memory_space=pltpu.SMEM)
    hbm = pl.BlockSpec(memory_space=pl.ANY)

    copies = 2 * n_row + n_chip
    query_range, keys, values, edge_values = pl.pallas_call(
        functools.partial(exchange, n_row, n_chip),
        out_shape=(
            jax.ShapeDtypeStruct((n_col, tile, width), bf16),
            jax.ShapeDtypeStruct((n_row, tile, width), bf16),
            jax.ShapeDtypeStruct((n_row, width, tile), bf16),
            jax.ShapeDtypeStruct((n_row,) + edge_weight.shape[3:], edge_weight.dtype),
        ),
        in_specs=[vmem] * 3 + [hbm] * 2,
        out_specs=(hbm, vmem, vmem, hbm),
        scratch_shapes=[
            pltpu.VMEM((tile, width), bf16),
            pltpu.VMEM((tile, width), bf16),
            pltpu.VMEM((n_row, tile, width), bf16),
            pltpu.VMEM(w_query.shape, bf16),
            pltpu.VMEM(w_keyvalue.shape, bf16),
            pltpu.SemaphoreType.DMA((copies,)),
            pltpu.SemaphoreType.DMA((copies,)),
            pltpu.SemaphoreType.DMA((n_chip,)),
            pltpu.SemaphoreType.DMA((n_chip, 2)),
            pltpu.SemaphoreType.DMA((4,)),
        ],
        compiler_params=pltpu.CompilerParams(
            collective_id=0, has_side_effects=True, vmem_limit_bytes=VMEM_LIMIT
        ),
        name="exchange",
    )(node_features, norm_gain[None], edge_weight[0, 0], w_query, w_keyvalue)
    partial_out, partial_level = pl.pallas_call(
        functools.partial(attend, slot_cap, dim ** (-0.5)),
        out_shape=(
            jax.ShapeDtypeStruct((n_col, width, tile), bf16),
            jax.ShapeDtypeStruct((n_col, heads, tile), f32),
        ),
        in_specs=[smem, smem, vmem] + [hbm] * 5,
        out_specs=(hbm, vmem),
        scratch_shapes=[
            pltpu.VMEM((n_col, heads, tile), f32),
            pltpu.VMEM((n_col, heads, tile), f32),
            pltpu.VMEM((n_col, heads, dim, tile), f32),
            pltpu.VMEM((heads, tile), f32),
            pltpu.VMEM((heads, tile, tile), f32),
            pltpu.VMEM(query_range.shape, bf16),
            pltpu.VMEM(keys.shape, bf16),
            pltpu.VMEM(values.shape, bf16),
            pltpu.VMEM((slots, tile, tile), bf16),
            pltpu.VMEM((slots, tile, tile), jnp.int32),
            pltpu.VMEM((n_col, width, tile), bf16),
            pltpu.SemaphoreType.DMA((3,)),
            pltpu.SemaphoreType.DMA((2, slots)),
            pltpu.SemaphoreType.DMA((n_col,)),
        ],
        compiler_params=pltpu.CompilerParams(vmem_limit_bytes=VMEM_LIMIT),
        name="attend",
    )(
        pair_blocks.reshape(2, slots),
        edge_slope,
        bias_table.T,
        query_range,
        keys,
        values,
        edge_values.reshape(slots, tile, tile),
        bucket_ids.reshape(slots, tile, tile),
    )
    attention = pl.pallas_call(
        functools.partial(combine, n_chip),
        out_shape=jax.ShapeDtypeStruct((width, tile), bf16),
        in_specs=[hbm, vmem],
        out_specs=vmem,
        scratch_shapes=[
            pltpu.VMEM((n_chip, width, tile), bf16),
            pltpu.VMEM((n_chip, heads, tile), f32),
        ]
        * 3
        + [pltpu.VMEM((n_chip, width, tile), bf16)]
        + [pltpu.SemaphoreType.DMA((4 * n_chip,))] * 2
        + [pltpu.SemaphoreType.DMA((n_chip,))],
        compiler_params=pltpu.CompilerParams(
            collective_id=1, has_side_effects=True, vmem_limit_bytes=VMEM_LIMIT
        ),
        name="combine",
    )(partial_out, partial_level)
    update = lax.dot_general(
        attention, w_out, (((0,), (0,)), ((), ())), preferred_element_type=f32
    )
    return (node_features.astype(f32) + update).astype(bf16)


def solution(mesh):
    return jax.shard_map(
        functools.partial(local, mesh.shape["row"], mesh.shape["col"]),
        mesh=mesh,
        in_specs=(
            P(("row", "col"), None),
            P(),
            P(),
            P(),
            P(),
            P(),
            P(),
            P("row", "col", None, None),
            P("row", "col", None, None, None),
            P("row", "col", None, None, None, None),
        ),
        out_specs=P(("row", "col"), None),
        check_vma=False,
    )
```

```python
import functools

import jax
import jax.numpy as jnp
from jax import lax
from jax.experimental import pallas as pl
from jax.experimental.pallas import tpu as pltpu
from jax.sharding import PartitionSpec as P

EPSILON = 1e-05
LOW_FLOOR = -1e30
CORES = 2
MESH = pl.DeviceIdType.MESH
LANES = 128
ROOM = 6 * 2**20


def normalize(features, gain_vec):
    as_float = features.astype(jnp.float32)
    centered = as_float - jnp.mean(as_float, axis=-1, keepdims=True)
    variance = jnp.mean(centered * centered, axis=-1, keepdims=True)
    return (centered * lax.rsqrt(variance + EPSILON) * gain_vec).astype(jnp.bfloat16)


def greet(partners):
    barrier = pltpu.get_barrier_semaphore()
    for partner in partners:
        pl.semaphore_signal(barrier, inc=1, device_id=partner, device_id_type=MESH)
    pl.semaphore_wait(barrier, len(partners))


def exchange(
    n_row, n_chip, x_in, gain_in, e_in, wq_in, w_in, q_out, k_out, v_out, e_out,
    q_in, n_in, n_buf, wq_buf, w_buf, send_sem, recv_sem, chip_sem, line_sem, own_sem,
):
    row, col = lax.axis_index("row"), lax.axis_index("col")
    chip, core = col // CORES, col % CORES
    sibling = (row, chip * CORES + (1 - core))
    chips = [(row, ((chip + k) % n_chip) * CORES + core) for k in range(1, n_chip)]
    rows = [((row + k) % n_row, col) for k in range(1, n_row)]
    width = n_in.shape[1]
    query_weights = pltpu.make_async_copy(wq_in, wq_buf, own_sem.at[3])
    weights = pltpu.make_async_copy(w_in, w_buf, own_sem.at[2])
    query_weights.start()
    greet(chips + [sibling] + rows)

    def remote(src, dst, send, recv, where):
        return pltpu.make_async_remote_copy(
            src_ref=src,
            dst_ref=dst,
            send_sem=send,
            recv_sem=recv,
            device_id=where,
            device_id_type=MESH,
        )

    def hop(step, way):
        origin = chip - way * step
        spot = origin * CORES + core
        copy = remote(
            q_in if step == 0 else q_out.at[spot],
            q_out.at[spot],
            line_sem.at[step, (way + 1) // 2],
            chip_sem.at[origin],
            (row, (chip + way) * CORES + core),
        )
        onward = (chip + way >= 0) & (chip + way < n_chip)
        return copy, onward, (origin >= 0) & (origin < n_chip), spot, origin

    weights.start()
    e_send = [
        remote(
            e_in.at[where[0]], e_out.at[row], send_sem.at[n_row + k], recv_sem.at[n_row + k], where
        )
        for k, where in enumerate(rows, 1)
    ]
    n_in[...] = normalize(x_in[...], gain_in[...])
    query_weights.wait()
    n_send = [
        remote(n_in, n_buf.at[k], send_sem.at[k], recv_sem.at[k], where)
        for k, where in enumerate(rows, 1)
    ]
    chunk = 2 * LANES

    @pl.loop(0, width // chunk)
    def _(step):
        left = pl.multiple_of(step * chunk, chunk)
        q_in[:, pl.ds(left, chunk)] = jnp.dot(
            n_in[...], wq_buf[:, pl.ds(left, chunk)], preferred_element_type=jnp.float32
        ).astype(q_in.dtype)

    for copy in n_send:
        copy.start()
    for way in (1, -1):
        copy, onward, _, _, _ = hop(0, way)

        @pl.when(onward)
        def _():
            copy.start()

    for copy in e_send:
        copy.start()
    pair_send = remote(q_in, q_out.at[col], send_sem.at[0], recv_sem.at[0], sibling)
    pair_send.start()
    own = [
        pltpu.make_async_copy(q_in, q_out.at[col], own_sem.at[0]),
        pltpu.make_async_copy(e_in.at[row], e_out.at[row], own_sem.at[1]),
    ]
    for copy in own:
        copy.start()

    def project(rows_ref, spot):
        hidden = rows_ref[...]

        @pl.loop(0, width // chunk)
        def _(step):
            left = pl.multiple_of(step * chunk, chunk)
            k_out[spot, :, pl.ds(left, chunk)] = jnp.dot(
                hidden, w_buf[:, pl.ds(left, chunk)], preferred_element_type=jnp.float32
            ).astype(k_out.dtype)
            right = pl.multiple_of(width + left, chunk)
            value = jnp.dot(hidden, w_buf[:, pl.ds(right, chunk)], preferred_element_type=jnp.float32)
            v_out[spot, pl.ds(left, chunk), :] = value.T.astype(v_out.dtype)

    weights.wait()
    project(n_in, row)

    def pass_on(step):
        for way in (1, -1):
            copy, onward, real, spot, origin = hop(step, way)

            @pl.when(real)
            def _():
                arrived = q_out.at[spot]
                copy.wait_recv()
                remote(
                    arrived,
                    arrived,
                    send_sem.at[2 * n_row + origin],
                    recv_sem.at[2 * n_row + origin],
                    sibling,
                ).start()

            if step < n_chip - 1:

                @pl.when(real & onward)
                def _():
                    hop(step, way)[0].start()

    for k in range(1, max(n_row, n_chip)):
        if k < n_chip:
            pass_on(k)
        if k < n_row:
            n_send[k - 1].wait_recv()
            project(n_buf.at[k], (row + n_row - k) % n_row)

    for way in (1, -1):
        for step in range(n_chip - 1):
            copy, onward, real, _, _ = hop(step, way)

            @pl.when(real & onward)
            def _():
                copy.wait_send()

        for step in range(1, n_chip):
            _, _, real, spot, origin = hop(step, way)

            @pl.when(real)
            def _():
                remote(
                    q_out.at[spot],
                    q_out.at[spot],
                    send_sem.at[2 * n_row + origin],
                    recv_sem.at[2 * n_row + origin],
                    sibling,
                ).wait()

    for copy in n_send:
        copy.wait_send()
    for copy in e_send + [pair_send]:
        copy.wait()
    for copy in own:
        copy.wait()


def attend(
    slot_cap, scale, pairs, slope, bias_ref, q_ref, k_ref, v_ref, e_ref, b_ref, o_ref, l_ref,
    m_acc, s_acc, o_acc, table, scores,
):
    query_count, heads, tile = l_ref.shape
    dim = q_ref.shape[2] // heads
    buckets_in = bias_ref.shape[1]
    m_acc[...] = jnp.full(m_acc.shape, LOW_FLOOR, jnp.float32)
    s_acc[...] = jnp.zeros(s_acc.shape, jnp.float32)
    o_acc[...] = jnp.zeros(o_acc.shape, jnp.float32)
    table[...] = jnp.zeros(table.shape, jnp.float32)
    table[:, :buckets_in] = bias_ref[...]

    def slot_step(slot, carry):
        query = pairs[0, slot]

        @pl.when(query >= 0)
        def _():
            key = pairs[1, slot] + slot // slot_cap
            buckets = b_ref[slot].T
            edges = e_ref[slot].astype(jnp.float32).T
            tops = []
            for h in range(heads):
                cols = slice(h * dim, (h + 1) * dim)
                score = lax.dot_general(
                    k_ref[key, :, cols],
                    q_ref[query, :, cols],
                    (((1,), (1,)), ((), ())),
                    preferred_element_type=jnp.float32,
                )
                entries = jnp.broadcast_to(table[h : h + 1, :], (tile, tile))
                bias = jnp.take_along_axis(entries, buckets, axis=1, mode="promise_in_bounds")
                score = score * scale + bias + slope[h] * edges
                scores[h] = score
                tops.append(jnp.max(score, axis=0, keepdims=True))
            old_max = m_acc[query]
            new_max = jnp.maximum(old_max, jnp.concatenate(tops, axis=0))
            keep = jnp.exp(old_max - new_max)
            m_acc[query] = new_max
            sums = []
            for h in range(heads):
                probs = jnp.exp(scores[h] - new_max[h : h + 1]).astype(jnp.bfloat16)
                sums.append(jnp.sum(probs.astype(jnp.float32), axis=0, keepdims=True))
                scores[h] = jnp.dot(
                    v_ref[key, h * dim : (h + 1) * dim, :], probs, preferred_element_type=jnp.float32
                )
            s_acc[query] = s_acc[query] * keep + jnp.concatenate(sums, axis=0)
            for h in range(heads):
                o_acc[query, h] = o_acc[query, h] * keep[h : h + 1] + scores[h]

        return carry

    lax.fori_loop(0, pairs.shape[1], slot_step, 0)

    def finish(query, carry):
        total = s_acc[query]
        live = total > 0.0
        safe = jnp.where(live, total, 1.0)
        l_ref[query] = jnp.where(live, m_acc[query] + jnp.log(safe), LOW_FLOOR)
        share = 1.0 / safe
        for h in range(heads):
            o_ref[query, h * dim : (h + 1) * dim, :] = (o_acc[query, h] * share[h : h + 1]).astype(
                o_ref.dtype
            )
        return carry

    lax.fori_loop(0, query_count, finish, 0)


def blend(levels, parts, heads):
    top = functools.reduce(jnp.maximum, levels)
    shares = [jnp.exp(level - top) for level in levels]
    total = functools.reduce(jnp.add, shares)
    weights = [share / total for share in shares]
    dim = parts[0].shape[0] // heads
    out = []
    for h in range(heads):
        rows = slice(h * dim, (h + 1) * dim)
        terms = [w[h : h + 1] * part[rows].astype(jnp.float32) for w, part in zip(weights, parts)]
        out.append(functools.reduce(jnp.add, terms))
    return out, top + jnp.log(total)


def partner(chip, k, n_chip):
    if n_chip & (n_chip - 1):
        return (chip + k) % n_chip
    bits = [1 << b for b in range(n_chip.bit_length() - 1)]
    return sum(((chip // bit + k // bit) % 2) * bit for bit in bits)


def combine(
    n_chip, o_ref, l_ref, a_ref, sib_o, sib_l, mix_o, mix_l, got_o, got_l, send_sem, recv_sem
):
    row, col = lax.axis_index("row"), lax.axis_index("col")
    chip, core = col // CORES, col % CORES
    heads = l_ref.shape[1]
    dim = o_ref.shape[1] // heads
    sibling = (row, chip * CORES + (1 - core))
    chips = [(row, partner(chip, k, n_chip) * CORES + core) for k in range(1, n_chip)]
    greet(chips + [sibling])

    def send(spot, src, dst, where):
        copy = pltpu.make_async_remote_copy(
            src_ref=src,
            dst_ref=dst,
            send_sem=send_sem.at[spot],
            recv_sem=recv_sem.at[spot],
            device_id=where,
            device_id_type=MESH,
        )
        copy.start()
        return copy

    half = n_chip // 2
    far = list(range(half, n_chip)) + list(range(1, half))
    order = far + [0]
    to_sibling = {}
    for k in order:
        theirs = partner(chip, k, n_chip) * CORES + (1 - core)
        to_sibling[k] = [
            send(4 * k, l_ref.at[theirs], sib_l.at[k], sibling),
            send(4 * k + 1, o_ref.at[theirs], sib_o.at[k], sibling),
        ]
    over = []

    def push(k):
        over.append(send(4 * k + 2, mix_l.at[k], got_l.at[k], chips[k - 1]))
        over.append(send(4 * k + 3, mix_o.at[k], got_o.at[k], chips[k - 1]))

    for k in far:
        for copy in to_sibling[k]:
            copy.wait_recv()
        mine = partner(chip, k, n_chip) * CORES + core
        out, level = blend([l_ref[mine], sib_l[k]], [o_ref[mine], sib_o[k]], heads)
        for h in range(heads):
            mix_o[k, h * dim : (h + 1) * dim, :] = out[h].astype(mix_o.dtype)
        mix_l[k] = level
        push(k)
    for copy in to_sibling[0]:
        copy.wait_recv()
    for copy in over:
        copy.wait_recv()
    levels = [l_ref[col], sib_l[0]] + [got_l[k] for k in range(1, n_chip)]
    parts = [o_ref[col], sib_o[0]] + [got_o[k] for k in range(1, n_chip)]
    out, _ = blend(levels, parts, heads)
    for h in range(heads):
        a_ref[h * dim : (h + 1) * dim, :] = out[h].astype(a_ref.dtype)
    for copies in to_sibling.values():
        for copy in copies:
            copy.wait_send()
    for copy in over:
        copy.wait_send()


def local(
    n_row,
    n_col,
    node_features,
    norm_gain,
    w_query,
    w_keyvalue,
    w_out,
    bias_table,
    edge_slope,
    pair_blocks,
    bucket_ids,
    edge_weight,
):
    tile, width = node_features.shape
    heads = edge_slope.shape[0]
    dim = width // heads
    n_chip = n_col // CORES
    slot_cap = edge_weight.shape[3]
    slots = n_row * slot_cap
    bf16, f32 = jnp.bfloat16, jnp.float32
    vmem = pl.BlockSpec(memory_space=pltpu.VMEM)
    smem = pl.BlockSpec(memory_space=pltpu.SMEM)
    hbm = pl.BlockSpec(memory_space=pl.ANY)

    block = 2 * tile * width
    weight_bytes = 2 * (w_query.size + w_keyvalue.size)
    exchange_bytes = (3 * n_row + 4) * block + weight_bytes + 2 * edge_weight.size
    attend_bytes = (4 * n_col + 2 * n_row) * block + 6 * slots * tile * tile
    combine_bytes = (n_col + 3 * n_chip + 2) * block
    copies = 2 * n_row + n_chip
    query_range, keys, values, edge_values = pl.pallas_call(
        functools.partial(exchange, n_row, n_chip),
        out_shape=(
            jax.ShapeDtypeStruct((n_col, tile, width), bf16),
            jax.ShapeDtypeStruct((n_row, tile, width), bf16),
            jax.ShapeDtypeStruct((n_row, width, tile), bf16),
            jax.ShapeDtypeStruct((n_row,) + edge_weight.shape[3:], edge_weight.dtype),
        ),
        in_specs=[vmem] * 3 + [hbm] * 2,
        out_specs=(hbm, vmem, vmem, hbm),
        scratch_shapes=[
            pltpu.VMEM((tile, width), bf16),
            pltpu.VMEM((tile, width), bf16),
            pltpu.VMEM((n_row, tile, width), bf16),
            pltpu.VMEM(w_query.shape, bf16),
            pltpu.VMEM(w_keyvalue.shape, bf16),
            pltpu.SemaphoreType.DMA((copies,)),
            pltpu.SemaphoreType.DMA((copies,)),
            pltpu.SemaphoreType.DMA((n_chip,)),
            pltpu.SemaphoreType.DMA((n_chip, 2)),
            pltpu.SemaphoreType.DMA((4,)),
        ],
        compiler_params=pltpu.CompilerParams(
            collective_id=0, has_side_effects=True, vmem_limit_bytes=exchange_bytes + ROOM
        ),
        name="exchange",
    )(node_features, norm_gain[None], edge_weight[0, 0], w_query, w_keyvalue)
    partial_out, partial_level = pl.pallas_call(
        functools.partial(attend, slot_cap, dim ** (-0.5)),
        out_shape=(
            jax.ShapeDtypeStruct((n_col, width, tile), bf16),
            jax.ShapeDtypeStruct((n_col, heads, tile), f32),
        ),
        in_specs=[smem, smem] + [vmem] * 6,
        out_specs=(vmem, vmem),
        scratch_shapes=[
            pltpu.VMEM((n_col, heads, tile), f32),
            pltpu.VMEM((n_col, heads, tile), f32),
            pltpu.VMEM((n_col, heads, dim, tile), f32),
            pltpu.VMEM((heads, tile), f32),
            pltpu.VMEM((heads, tile, tile), f32),
        ],
        compiler_params=pltpu.CompilerParams(vmem_limit_bytes=attend_bytes + ROOM),
        name="attend",
    )(
        pair_blocks.reshape(2, slots),
        edge_slope,
        bias_table.T,
        query_range,
        keys,
        values,
        edge_values.reshape(slots, tile, tile),
        bucket_ids.reshape(slots, tile, tile),
    )
    attention = pl.pallas_call(
        functools.partial(combine, n_chip),
        out_shape=jax.ShapeDtypeStruct((width, tile), bf16),
        in_specs=[vmem] * 2,
        out_specs=vmem,
        scratch_shapes=[
            pltpu.VMEM((n_chip, width, tile), bf16),
            pltpu.VMEM((n_chip, heads, tile), f32),
        ]
        * 3
        + [pltpu.SemaphoreType.DMA((4 * n_chip,))] * 2,
        compiler_params=pltpu.CompilerParams(
            collective_id=1, has_side_effects=True, vmem_limit_bytes=combine_bytes + ROOM
        ),
        name="combine",
    )(partial_out, partial_level)
    update = lax.dot_general(
        attention, w_out, (((0,), (0,)), ((), ())), preferred_element_type=f32
    )
    return (node_features.astype(f32) + update).astype(bf16)


def solution(mesh):
    return jax.shard_map(
        functools.partial(local, mesh.shape["row"], mesh.shape["col"]),
        mesh=mesh,
        in_specs=(
            P(("row", "col"), None),
            P(),
            P(),
            P(),
            P(),
            P(),
            P(),
            P("row", "col", None, None),
            P("row", "col", None, None, None),
            P("row", "col", None, None, None, None),
        ),
        out_specs=P(("row", "col"), None),
        check_vma=False,
    )
```
